32 devices in a mesh: stn: 8 (over z, x), grp: 4 (over y, core).
Axes of the slice: x: 2, y: 2, z: 4, core: 2. Of those that a mesh axis runs over, the one named last changes fastest.
Arguments:
- voltages: bfloat16 [2, 16, 2, 180224], P(None, 'stn', None, 'grp'), may hold values from -6 to 6
- corr_taps: float32 [12, 4096], replicated, may hold values from -1.75 to 1.75
- beam_taps: float32 [12, 256], replicated, may hold values from -1.75 to 1.75
- angle_table: float32 [64, 256], replicated, may hold values from -3.140625 to 3.140625
- table_index: int32 [16, 16], replicated, may hold values from 0 to 63
Outputs:
- visibility: float32 [8, 32, 2, 32], P('stn', 'grp')
- beam_power: float32 [256, 16, 704], P('stn', None, 'grp')
The draws below stay inside these ranges and needn't reach their ends.
All inputs are finite; a program needn't handle non-finite values.
Results may differ from the reference program's by a relative error of at most 0.0046.
Values may be sent and summed in bfloat16 or wider, within the bound.
No kernel may reach another device: no remote copies, remote signals or barrier semaphores. Data moves between devices by JAX's collectives and lax.ppermute only.
A program may use at most 128 MiB of HBM per device.

```python
import math
import jax
import jax.numpy as jnp
from jax import lax

S_DEV = 2
RADIX = 64
TAPS = 12
CH_B = 256
BEAMS = 16
TABLE = 64
STATIONS = 16
SIG = 32
CH = 4096
TIME = 180224
BIN_CH = 512
N_STN = 8


def plant(result, stream_key, smallest, high):
    shape = result.shape
    place = [jax.random.randint(jax.random.fold_in(stream_key, axis), (), 0, shape[axis]) for axis in range(len(shape))]
    result = result.at[tuple(place)].set(smallest)
    longest = shape.index(max(shape))
    place[longest] = (place[longest] + 1) % shape[longest]
    return result.at[tuple(place)].set(high)


def level_of(key, dims, pieces, smallest, high):
    loudness = 1.0
    for axis_at, shards_of in pieces:
        draws = jax.random.uniform(jax.random.fold_in(jax.random.fold_in(key, 6), axis_at), (shards_of,), jnp.float32, smallest / len(pieces), high / len(pieces))
        loudness = loudness * jnp.repeat(jnp.exp(draws), dims[axis_at] // shards_of).reshape((-1,) + (1,) * (len(dims) - 1 - axis_at))
    return loudness


def normal_values(own_key, extent, width, limit, cuts=(), kind=jnp.bfloat16):
    array = width * jax.random.normal(own_key, extent, jnp.float32)
    if cuts:
        array = array * level_of(own_key, extent, cuts, -0.22, 0.18)
    return jnp.clip(array, -limit, limit).astype(kind)


def setup_inputs(seed: int = 0) -> dict:
    key_of = jax.random.split(jax.random.key(seed), 6)
    voltages = normal_values(key_of[0], (2, STATIONS, 2, TIME), 1.0, 6.0, ((1, 8), (3, 4)))
    corr_taps = normal_values(key_of[1], (TAPS, CH), TAPS ** -0.5, 1.75, (), jnp.float32)
    beam_taps = normal_values(key_of[2], (TAPS, CH_B), TAPS ** -0.5, 1.75, (), jnp.float32)
    angle_table = jnp.clip(jax.random.uniform(key_of[3], (TABLE, CH_B), jnp.float32, -3.140625, 3.140625), -3.140625, 3.140625)
    table_index = plant(jax.random.randint(key_of[4], (BEAMS, STATIONS), 0, TABLE), jax.random.fold_in(key_of[4], 1), 0, TABLE - 1).astype(jnp.int32)
    return dict(voltages=voltages, corr_taps=corr_taps, beam_taps=beam_taps, angle_table=angle_table, table_index=table_index)


def dft_tables(length):
    positions = jnp.arange(length, dtype=jnp.int32)
    phases = (positions[:, None] * positions[None, :] % length).astype(jnp.float32) * (2.0 * math.pi / length)
    factor = 1.0 / math.sqrt(length)
    return ((jnp.cos(phases) * factor).astype(jnp.bfloat16), (jnp.sin(phases) * factor).astype(jnp.bfloat16))

def twiddles(radix_size):
    positions = jnp.arange(radix_size, dtype=jnp.int32)
    whole = radix_size * radix_size
    phases = (positions[:, None] * positions[None, :] % whole).astype(jnp.float32) * (2.0 * math.pi / whole)
    return (jnp.cos(phases), jnp.sin(phases))

def polyphase(extended, coefficients, frame_count):
    tap_count, length = coefficients.shape
    shaped = extended.reshape(extended.shape[:-1] + (frame_count + tap_count - 1, length))
    summed = jnp.zeros(shaped.shape[:-2] + (frame_count, length), jnp.float32)
    for tap_index in range(tap_count):
        lead_frame = tap_count - 1 - tap_index
        summed = summed + shaped[..., lead_frame:lead_frame + frame_count, :].astype(jnp.float32) * coefficients[tap_index]
    return summed.astype(jnp.bfloat16)

def contract(pattern, left_side, right_side):
    return jnp.einsum(pattern, left_side.astype(jnp.float32), right_side.astype(jnp.float32), precision=lax.Precision.HIGHEST)

def long_transform(real_part, imag_part):
    cos_table, sin_table = dft_tables(RADIX)
    twist_cos, twist_sin = twiddles(RADIX)
    split_shape = real_part.shape[:-1] + (RADIX, RADIX)
    real_part = real_part.reshape(split_shape)
    imag_part = imag_part.reshape(split_shape)
    first_form = '...ab,ak->...kb'
    middle_real = contract(first_form, real_part, cos_table) + contract(first_form, imag_part, sin_table)
    middle_imag = contract(first_form, imag_part, cos_table) - contract(first_form, real_part, sin_table)
    twisted_real = (middle_real * twist_cos + middle_imag * twist_sin).astype(jnp.bfloat16)
    twisted_imag = (middle_imag * twist_cos - middle_real * twist_sin).astype(jnp.bfloat16)
    second_form = '...kb,bm->...mk'
    result_real = contract(second_form, twisted_real, cos_table) + contract(second_form, twisted_imag, sin_table)
    result_imag = contract(second_form, twisted_imag, cos_table) - contract(second_form, twisted_real, sin_table)
    flat_shape = split_shape[:-2] + (RADIX * RADIX,)
    return (result_real.astype(jnp.bfloat16).reshape(flat_shape), result_imag.astype(jnp.bfloat16).reshape(flat_shape))

def short_transform(real_part, imag_part):
    cos_table, sin_table = dft_tables(real_part.shape[-1])
    pattern = '...n,nk->...k'
    result_real = contract(pattern, real_part, cos_table) + contract(pattern, imag_part, sin_table)
    result_imag = contract(pattern, imag_part, cos_table) - contract(pattern, real_part, sin_table)
    return (result_real.astype(jnp.bfloat16), result_imag.astype(jnp.bfloat16))

def beam_terms(weight_real, weight_imag, spec_real, spec_imag):
    pattern = 'bsc,sptc->cpbt'
    real_part = contract(pattern, weight_real, spec_real) - contract(pattern, weight_imag, spec_imag)
    imag_part = contract(pattern, weight_real, spec_imag) + contract(pattern, weight_imag, spec_real)
    return jnp.stack([real_part, imag_part], 1)

def reference(voltages, corr_taps, beam_taps, angle_table, table_index):
    tap_count = corr_taps.shape[0]
    angles = jnp.take(angle_table, table_index, axis=0)
    factor = 1.0 / math.sqrt(STATIONS)
    weight_real = (jnp.cos(angles) * factor).astype(jnp.bfloat16)
    weight_imag = (jnp.sin(angles) * factor).astype(jnp.bfloat16)
    frames = TIME // CH
    short_frames = TIME // CH_B

    def station_block(running, first_station):
        station_data = lax.dynamic_slice_in_dim(voltages, first_station, S_DEV, 1)
        padded = jnp.pad(station_data, ((0, 0), (0, 0), (0, 0), ((tap_count - 1) * CH, 0)))
        filtered = polyphase(padded, corr_taps, frames)
        spec_real, spec_imag = long_transform(filtered[0], filtered[1])
        short_input = padded[..., (tap_count - 1) * (CH - CH_B):]
        short_filtered = polyphase(short_input, beam_taps, short_frames)
        beam_real, beam_imag = short_transform(short_filtered[0], short_filtered[1])
        part_real = lax.dynamic_slice_in_dim(weight_real, first_station, S_DEV, 1)
        part_imag = lax.dynamic_slice_in_dim(weight_imag, first_station, S_DEV, 1)
        running = running + beam_terms(part_real, part_imag, beam_real, beam_imag)
        return (running, (spec_real, spec_imag))
    starts = jnp.arange(N_STN, dtype=jnp.int32) * S_DEV
    initial = jnp.zeros((CH_B, 2, 2, BEAMS, short_frames), jnp.float32)
    beam_fields, (spec_real, spec_imag) = lax.scan(station_block, initial, starts)
    spec_real = spec_real.reshape(SIG, frames, CH)
    spec_imag = spec_imag.reshape(SIG, frames, CH)

    def one_bin(first_channel):
        part_real = lax.dynamic_slice_in_dim(spec_real, first_channel, BIN_CH, 2).reshape(SIG, frames * BIN_CH)
        part_imag = lax.dynamic_slice_in_dim(spec_imag, first_channel, BIN_CH, 2).reshape(SIG, frames * BIN_CH)
        stacked = jnp.concatenate([part_real, part_imag], 1)
        rotated = jnp.concatenate([part_imag, -part_real], 1)
        real_part = jnp.dot(stacked, stacked.T, preferred_element_type=jnp.float32)
        imag_part = jnp.dot(rotated, stacked.T, preferred_element_type=jnp.float32)
        return jnp.stack([real_part, imag_part], 1)
    summed = lax.map(one_bin, jnp.arange(N_STN, dtype=jnp.int32) * BIN_CH)
    visibility = summed * (1.0 / math.sqrt(frames * BIN_CH))
    beam_power = lax.optimization_barrier(jnp.sum(beam_fields[:, 0] ** 2 + beam_fields[:, 1] ** 2, axis=1))
    return (visibility, beam_power)
```

```python
import functools
import math

import jax
import jax.numpy as jnp
import numpy as np
from jax import lax
from jax.experimental import pallas as pl
from jax.experimental.pallas import tpu as pltpu
from jax.sharding import PartitionSpec as P

LANES = 128
GROUPS = 8


def from_behind(array, axis, by):
    devices = lax.axis_size(axis)
    pairs = [(i, i + by) for i in range(devices) if 0 <= i + by < devices]
    return lax.ppermute(array, axis, pairs)


def dft_tables(rows, columns):
    length = max(rows, columns)
    phases = (np.arange(rows)[:, None] * np.arange(columns)[None, :] % length) * (2.0 * np.pi / length)
    return np.cos(phases) / math.sqrt(length), np.sin(phases) / math.sqrt(length)


def pulsar_table(length):
    cos_table, sin_table = dft_tables(length, length)
    return np.concatenate([cos_table, sin_table], 1)


def block_stage_table(blocks, pairs):
    cos_table, sin_table = dft_tables(blocks, blocks)
    real_row = np.stack([cos_table, sin_table], 0)
    imag_row = np.stack([-sin_table, cos_table], 0)
    parts = np.stack([np.stack([real_row, imag_row], 0), np.stack([imag_row, -real_row], 0)], 0)
    parts = parts.reshape(2, 2, 2, blocks, blocks // GROUPS, GROUPS)
    full = np.einsum("aorbqi,sp->aiqosrpb", parts, np.eye(pairs))
    return full.reshape(2 * blocks * 2 * pairs, 2 * pairs * blocks)


def lane_stage_table():
    cos_table, sin_table = dft_tables(LANES, LANES)
    table = np.concatenate([cos_table, sin_table], 0)
    width = LANES // GROUPS
    return np.concatenate([np.roll(table, i * width, 1) for i in range(GROUPS)], 1)


def twiddle_tables(blocks, repeats):
    order = np.arange(blocks).reshape(blocks // GROUPS, GROUPS).T.reshape(-1)
    phases = (order[:, None] * np.arange(LANES)[None, :]) * (2.0 * np.pi / (blocks * LANES))
    phases = np.repeat(phases, repeats, 0)
    return np.cos(phases).astype(np.float32), np.sin(phases).astype(np.float32)


def dot(left_side, right_side):
    return jnp.dot(left_side, right_side, preferred_element_type=jnp.float32)


def dot_rows(left_side, right_side):
    return lax.dot_general(
        left_side, right_side, (((1,), (1,)), ((), ())), preferred_element_type=jnp.float32
    )


def pulsar_kernel(history_ref, own_ref, taps_ref, table_ref, out_ref, wide, summed, stacked):
    rows = own_ref.shape[0]
    taps, length = taps_ref.shape
    parts = length // LANES
    frames = own_ref.shape[1] // length
    past = history_ref.shape[1] // LANES
    for block in range(past):
        wide[block] = history_ref[:, block * LANES : (block + 1) * LANES].astype(jnp.float32)

    def widen(step, carry):
        at = pl.multiple_of(step * (16 * LANES), 16 * LANES)
        piece = own_ref[:, pl.ds(at, 16 * LANES)]
        for j in range(16):
            wide[past + step * 16 + j] = piece[:, j * LANES : (j + 1) * LANES].astype(jnp.float32)
        return carry

    lax.fori_loop(0, own_ref.shape[1] // LANES // 16, widen, 0)
    chunk = 16
    for part in range(parts):
        weights = [
            jnp.broadcast_to(taps_ref[k : k + 1, part * LANES : (part + 1) * LANES], (rows, LANES))
            for k in range(taps)
        ]

        def filter_frames(step, carry):
            first = step * chunk
            values = [wide[(first + j) * parts + part] for j in range(chunk + taps - 1)]
            for j in range(chunk):
                total = values[j + taps - 1] * weights[0]
                for k in range(1, taps):
                    total = total + values[j + taps - 1 - k] * weights[k]
                summed[part, pl.ds(first + j, rows, stride=frames), :] = total
            return carry

        lax.fori_loop(0, frames // chunk, filter_frames, 0)
    half = rows * frames // 2

    def stack(step, carry):
        at = pl.multiple_of(step * 64, 64)
        for part in range(parts):
            real_part = summed[part, pl.ds(at, 64), :].astype(jnp.bfloat16)
            imag_part = summed[part, pl.ds(at + half, 64), :].astype(jnp.bfloat16)
            low = slice(part * LANES, (part + 1) * LANES)
            high = slice(length + part * LANES, length + (part + 1) * LANES)
            stacked[pl.ds(at, 64), low] = real_part
            stacked[pl.ds(at, 64), high] = imag_part
            stacked[pl.ds(at + half, 64), low] = imag_part
            stacked[pl.ds(at + half, 64), high] = -real_part
        return carry

    lax.fori_loop(0, half // 64, stack, 0)
    out_ref[...] = dot_rows(table_ref[...], stacked[...]).astype(jnp.bfloat16)


def pulsar_spectra(history, own, taps):
    rows, samples = own.shape
    length = taps.shape[1]
    frames = samples // length
    table = jnp.asarray(pulsar_table(length), jnp.bfloat16)
    blocks = (history.shape[1] + samples) // LANES
    return pl.pallas_call(
        pulsar_kernel,
        out_shape=jax.ShapeDtypeStruct((length, rows * frames), jnp.bfloat16),
        scratch_shapes=[
            pltpu.VMEM((blocks, rows, LANES), jnp.float32),
            pltpu.VMEM((length // LANES, rows * frames, LANES), jnp.float32),
            pltpu.VMEM((rows * frames, 2 * length), jnp.bfloat16),
        ],
        cost_estimate=pl.CostEstimate(flops=600000000, bytes_accessed=2000000, transcendentals=0),
        name="pulsar_spectra",
    )(history, own, taps, table)


def correlator_kernel(history_ref, own_ref, taps_ref, first_ref, second_ref, cos_ref, sin_ref, out_ref, wide, summed, twisted, mixed):
    rows = own_ref.shape[0]
    taps, length = taps_ref.shape
    blocks = length // LANES
    frames = own_ref.shape[1] // length
    past = taps - 1
    for ref, start in ((history_ref, 0), (own_ref, past * blocks)):

        def widen(step, carry, ref=ref, start=start):
            at = pl.multiple_of(step * (16 * LANES), 16 * LANES)
            piece = ref[:, pl.ds(at, 16 * LANES)]
            for j in range(16):
                wide[start + step * 16 + j] = piece[:, j * LANES : (j + 1) * LANES].astype(jnp.float32)
            return carry

        lax.fori_loop(0, ref.shape[1] // LANES // 16, widen, 0)

    def filter_block(block, carry):
        at = pl.multiple_of(block * LANES, LANES)
        weights = [
            jnp.broadcast_to(taps_ref[k : k + 1, pl.ds(at, LANES)], (rows, LANES)) for k in range(taps)
        ]
        values = [wide[frame * blocks + block] for frame in range(frames + past)]
        for frame in range(frames):
            total = values[frame + past] * weights[0]
            for k in range(1, taps):
                total = total + values[frame + past - k] * weights[k]
            summed[frame, pl.ds(block, rows, stride=blocks), :] = total
        return carry

    lax.fori_loop(0, blocks, filter_block, 0)
    height = rows * blocks
    per_group = height // GROUPS

    def transform(frame, carry):
        middle = dot(first_ref[...], summed[frame].astype(jnp.bfloat16))
        left_part, right_part = middle[:height], middle[height:]
        twist_cos, twist_sin = cos_ref[...], sin_ref[...]
        low = (left_part * twist_cos + right_part * twist_sin).astype(jnp.bfloat16)
        high = (right_part * twist_cos - left_part * twist_sin).astype(jnp.bfloat16)
        at = pl.multiple_of(frame * per_group, per_group)
        for i in range(GROUPS):
            here = slice(i * per_group, (i + 1) * per_group)
            twisted[i, pl.ds(at, per_group), :LANES] = low[here]
            twisted[i, pl.ds(at, per_group), LANES:] = high[here]
        return carry

    lax.fori_loop(0, frames, transform, 0)
    for i in range(GROUPS):
        mixed[i] = dot(twisted[i], second_ref[:, i * LANES : (i + 1) * LANES])
    group = lax.broadcasted_iota(jnp.int32, (rows, LANES), 1) // (LANES // GROUPS)

    def gather(step, carry):
        at = pl.multiple_of(step * rows, rows)
        tiles = [mixed[i, pl.ds(at, rows), :] for i in range(GROUPS)]
        for bit in (1, 2, 4):
            pick = (group & bit) != 0
            tiles = [jnp.where(pick, tiles[(i + bit) % GROUPS], tiles[i]) for i in range(GROUPS)]
        lane = pl.multiple_of(step * LANES, LANES)
        for d in range(GROUPS):
            out_ref[d * rows : (d + 1) * rows, pl.ds(lane, LANES)] = tiles[-d % GROUPS].astype(jnp.bfloat16)
        return carry

    lax.fori_loop(0, frames * blocks // GROUPS, gather, 0)


def correlator_spectra(history, own, taps):
    rows, samples = own.shape
    length = taps.shape[1]
    frames = samples // length
    blocks = length // LANES
    first = jnp.asarray(block_stage_table(blocks, rows // 2), jnp.bfloat16)
    second = jnp.asarray(lane_stage_table(), jnp.bfloat16)
    twist_cos, twist_sin = twiddle_tables(blocks, rows)
    height = rows * blocks
    tiles = frames * blocks // GROUPS
    return pl.pallas_call(
        correlator_kernel,
        out_shape=jax.ShapeDtypeStruct((GROUPS * rows, tiles * LANES), jnp.bfloat16),
        scratch_shapes=[
            pltpu.VMEM(((frames + taps.shape[0] - 1) * blocks, rows, LANES), jnp.float32),
            pltpu.VMEM((frames, height, LANES), jnp.float32),
            pltpu.VMEM((GROUPS, frames * height // GROUPS, 2 * LANES), jnp.bfloat16),
            pltpu.VMEM((GROUPS, frames * height // GROUPS, LANES), jnp.float32),
        ],
        cost_estimate=pl.CostEstimate(flops=1000000000, bytes_accessed=4000000, transcendentals=0),
        name="correlator_spectra",
    )(history, own, taps, first, second, jnp.asarray(twist_cos), jnp.asarray(twist_sin))


def beam_kernel(weight_ref, spec_ref, out_ref, stacked):
    sources = spec_ref.shape[0]
    depth = weight_ref.shape[1]
    terms = depth // sources
    width = spec_ref.shape[1] // terms
    for i in range(terms):
        stacked[i * sources : (i + 1) * sources, :] = spec_ref[:, i * width : (i + 1) * width]
    height = weight_ref.shape[0] // 2
    chunk = min(height, 128)
    frames = width // 2

    def form(step, carry):
        at = pl.multiple_of(step * chunk, chunk)
        real_part = dot(weight_ref[pl.ds(at, chunk), :], stacked[...])
        imag_part = dot(weight_ref[pl.ds(height + at, chunk), :], stacked[...])
        power = real_part * real_part + imag_part * imag_part
        out_ref[pl.ds(at, chunk), :] = power[:, :frames] + power[:, frames:]
        return carry

    lax.fori_loop(0, height // chunk, form, 0)


def beam_former(weights, spectra):
    terms = weights.shape[1] // spectra.shape[0]
    width = spectra.shape[1] // terms
    return pl.pallas_call(
        beam_kernel,
        out_shape=jax.ShapeDtypeStruct((weights.shape[0] // 2, width // 2), jnp.float32),
        scratch_shapes=[pltpu.VMEM((weights.shape[1], width), jnp.bfloat16)],
        cost_estimate=pl.CostEstimate(flops=700000000, bytes_accessed=4000000, transcendentals=0),
        name="beam_former",
    )(weights, spectra)


def gram_kernel(spec_ref, out_ref):
    out_ref[...] = dot_rows(spec_ref[...], spec_ref[...])


def gram(spectra):
    rows = spectra.shape[0]
    return pl.pallas_call(
        gram_kernel,
        out_shape=jax.ShapeDtypeStruct((rows, rows), jnp.float32),
        cost_estimate=pl.CostEstimate(flops=50000000, bytes_accessed=1000000, transcendentals=0),
        name="gram",
    )(spectra)


def station_weights(index_rows, columns, station_total):
    table_rows = jnp.arange(columns.shape[0], dtype=jnp.int32)
    one_hot = (index_rows[..., None] == table_rows).astype(jnp.float32)
    angles = jnp.einsum("bst,tc->bsc", one_hot, columns, precision=lax.Precision.HIGHEST)
    factor = 1.0 / math.sqrt(station_total)
    return (
        (jnp.cos(angles) * factor).astype(jnp.bfloat16),
        (jnp.sin(angles) * factor).astype(jnp.bfloat16),
    )


def beam_matrix(weight_real, weight_imag, local_stations):
    beams, stations, channels = weight_real.shape
    parts = jnp.stack(
        [jnp.stack([weight_real, -weight_imag], 0), jnp.stack([weight_imag, weight_real], 0)], 0
    )
    parts = parts.reshape(2, 2, beams, stations // local_stations, local_stations, channels)
    parts = parts.transpose(0, 5, 2, 1, 4, 3)[..., None]
    same = jnp.eye(channels, dtype=jnp.bfloat16).reshape(1, channels, 1, 1, 1, 1, channels)
    return (parts * same).reshape(2 * channels * beams, 2 * stations * channels)


def sum_over_grp(matrix):
    members = lax.axis_size("grp")
    me = lax.axis_index("grp")
    blocks = matrix.reshape(members, matrix.shape[0] // members, matrix.shape[1])
    total = lax.dynamic_index_in_dim(blocks, me, 0, keepdims=False)
    for by in range(1, members):
        away = lax.dynamic_index_in_dim(blocks, (me + by) % members, 0, keepdims=False)
        total = total + lax.ppermute(away, "grp", [(i, (i + by) % members) for i in range(members)])
    return total


def on_device(voltages, corr_taps, beam_taps, angle_table, table_index):
    tap_count = corr_taps.shape[0]
    length = corr_taps.shape[1]
    short_length = beam_taps.shape[1]
    local_stations, polarizations, samples = voltages.shape[1:]
    owners = lax.axis_size("stn")
    station_total = local_stations * owners
    pairs = local_stations * polarizations
    rows = 2 * pairs
    own = voltages.reshape(rows, samples)
    short_past = (tap_count - 1) * short_length
    near = from_behind(own[:, samples - short_past :], "grp", 1)
    past = from_behind(own[:, samples - (tap_count - 1) * length :], "grp", 1)
    short = pulsar_spectra(near, own, beam_taps)
    owned_channels = short_length // owners
    short = short.reshape(owners, owned_channels, short.shape[1])
    short_turned = lax.all_to_all(short, "stn", split_axis=0, concat_axis=0, tiled=True)
    spectra = correlator_spectra(past, own, corr_taps)
    subs = owners // GROUPS
    spectra = spectra.reshape(GROUPS, rows, -1, subs, LANES // GROUPS // subs)
    spectra = spectra.transpose(0, 3, 1, 2, 4).reshape(owners, rows, -1)
    turned = lax.all_to_all(spectra, "stn", split_axis=0, concat_axis=0, tiled=True)
    columns = lax.dynamic_slice_in_dim(
        angle_table, lax.axis_index("stn") * owned_channels, owned_channels, 1
    )
    weight_real, weight_imag = station_weights(table_index, columns, station_total)
    matrix = beam_matrix(weight_real, weight_imag, local_stations)
    beam_power = beam_former(matrix, short_turned.reshape(owners * owned_channels, -1))
    beam_power = beam_power.reshape(owned_channels, table_index.shape[0], -1)
    inner_depth = turned.shape[2]
    products = gram(turned.reshape(owners * rows, inner_depth))
    summed = sum_over_grp(products)
    held = owners // lax.axis_size("grp")
    summed = summed.reshape(held, 2, pairs, owners, 2, pairs)
    real_part = summed[:, 0, :, :, 0] + summed[:, 1, :, :, 1]
    imag_part = summed[:, 1, :, :, 0] - summed[:, 0, :, :, 1]
    signals = owners * pairs
    visibility = jnp.stack(
        [real_part.reshape(held * pairs, signals), imag_part.reshape(held * pairs, signals)], 1
    )
    visibility = (visibility * (1.0 / math.sqrt(inner_depth * lax.axis_size("grp"))))[None]
    return (visibility, beam_power)


def solution(mesh):
    in_specs = (P(None, "stn", None, "grp"), P(), P(), P(), P())
    out_specs = (P("stn", "grp", None, None), P("stn", None, "grp"))
    return jax.shard_map(
        on_device, mesh=mesh, in_specs=in_specs, out_specs=out_specs, check_vma=False
    )
```

```python
import math

import jax
import jax.numpy as jnp
import numpy as np
from jax import lax
from jax.experimental import pallas as pl
from jax.experimental.pallas import tpu as pltpu
from jax.sharding import PartitionSpec as P

LANES = 128
GROUPS = 8
VMEM_BYTES = 24 * 1024 * 1024


def from_behind(array, axis, by):
    devices = lax.axis_size(axis)
    pairs = [(i, i + by) for i in range(devices) if 0 <= i + by < devices]
    return lax.ppermute(array, axis, pairs)


def dft_tables(rows, columns):
    length = max(rows, columns)
    phases = (np.arange(rows)[:, None] * np.arange(columns)[None, :] % length) * (2.0 * np.pi / length)
    return np.cos(phases) / math.sqrt(length), np.sin(phases) / math.sqrt(length)


def pulsar_table(length):
    cos_table, sin_table = dft_tables(length, length)
    return np.concatenate([cos_table, sin_table], 1)


def block_stage_table(blocks, pairs):
    cos_table, sin_table = dft_tables(blocks, blocks)
    real_row = np.stack([cos_table, sin_table], 0)
    imag_row = np.stack([-sin_table, cos_table], 0)
    parts = np.stack([np.stack([real_row, imag_row], 0), np.stack([imag_row, -real_row], 0)], 0)
    parts = parts.reshape(2, 2, 2, blocks, blocks // GROUPS, GROUPS)
    full = np.einsum("aorbqi,sp->aiqosrpb", parts, np.eye(pairs))
    return full.reshape(2 * blocks * 2 * pairs, 2 * pairs * blocks)


def lane_stage_table():
    cos_table, sin_table = dft_tables(LANES, LANES)
    table = np.concatenate([cos_table, sin_table], 0)
    width = LANES // GROUPS
    return np.concatenate([np.roll(table, i * width, 1) for i in range(GROUPS)], 1)


def twiddle_tables(blocks, repeats):
    order = np.arange(blocks).reshape(blocks // GROUPS, GROUPS).T.reshape(-1)
    phases = (order[:, None] * np.arange(LANES)[None, :]) * (2.0 * np.pi / (blocks * LANES))
    phases = np.repeat(phases, repeats, 0)
    return np.cos(phases).astype(np.float32), np.sin(phases).astype(np.float32)


def dot(left_side, right_side):
    return jnp.dot(left_side, right_side, preferred_element_type=jnp.float32)


def dot_rows(left_side, right_side):
    return lax.dot_general(
        left_side, right_side, (((1,), (1,)), ((), ())), preferred_element_type=jnp.float32
    )


def pulsar_kernel(history_ref, own_ref, taps_ref, table_ref, out_ref, wide, summed, stacked):
    rows = own_ref.shape[0]
    taps, length = taps_ref.shape
    parts = length // LANES
    frames = own_ref.shape[1] // length
    past = history_ref.shape[1] // LANES
    for block in range(past):
        wide[block] = history_ref[:, block * LANES : (block + 1) * LANES].astype(jnp.float32)

    def widen(step, carry):
        at = pl.multiple_of(step * (16 * LANES), 16 * LANES)
        piece = own_ref[:, pl.ds(at, 16 * LANES)]
        for j in range(16):
            wide[past + step * 16 + j] = piece[:, j * LANES : (j + 1) * LANES].astype(jnp.float32)
        return carry

    lax.fori_loop(0, own_ref.shape[1] // LANES // 16, widen, 0)
    chunk = 16
    for part in range(parts):
        weights = [
            jnp.broadcast_to(taps_ref[k : k + 1, part * LANES : (part + 1) * LANES], (rows, LANES))
            for k in range(taps)
        ]

        def filter_frames(step, carry):
            first = step * chunk
            values = [wide[(first + j) * parts + part] for j in range(chunk + taps - 1)]
            for j in range(chunk):
                total = values[j + taps - 1] * weights[0]
                for k in range(1, taps):
                    total = total + values[j + taps - 1 - k] * weights[k]
                summed[part, pl.ds(first + j, rows, stride=frames), :] = total
            return carry

        lax.fori_loop(0, frames // chunk, filter_frames, 0)
    half = rows * frames // 2

    def stack(step, carry):
        at = pl.multiple_of(step * 64, 64)
        for part in range(parts):
            real_part = summed[part, pl.ds(at, 64), :].astype(jnp.bfloat16)
            imag_part = summed[part, pl.ds(at + half, 64), :].astype(jnp.bfloat16)
            low = slice(part * LANES, (part + 1) * LANES)
            high = slice(length + part * LANES, length + (part + 1) * LANES)
            stacked[pl.ds(at, 64), low] = real_part
            stacked[pl.ds(at, 64), high] = imag_part
            stacked[pl.ds(at + half, 64), low] = imag_part
            stacked[pl.ds(at + half, 64), high] = -real_part
        return carry

    lax.fori_loop(0, half // 64, stack, 0)
    out_ref[...] = dot_rows(table_ref[...], stacked[...]).astype(jnp.bfloat16)


def pulsar_spectra(history, own, taps):
    rows, samples = own.shape
    length = taps.shape[1]
    frames = samples // length
    table = jnp.asarray(pulsar_table(length), jnp.bfloat16)
    blocks = (history.shape[1] + samples) // LANES
    return pl.pallas_call(
        pulsar_kernel,
        out_shape=jax.ShapeDtypeStruct((length, rows * frames), jnp.bfloat16),
        scratch_shapes=[
            pltpu.VMEM((blocks, rows, LANES), jnp.float32),
            pltpu.VMEM((length // LANES, rows * frames, LANES), jnp.float32),
            pltpu.VMEM((rows * frames, 2 * length), jnp.bfloat16),
        ],
        cost_estimate=pl.CostEstimate(flops=5000000000, bytes_accessed=2000000, transcendentals=0),
        compiler_params=pltpu.CompilerParams(vmem_limit_bytes=VMEM_BYTES),
        name="pulsar_spectra",
    )(history, own, taps, table)


def correlator_kernel(history_ref, own_ref, taps_ref, first_ref, second_ref, cos_ref, sin_ref, out_ref, wide, summed, twisted, mixed):
    rows = own_ref.shape[0]
    taps, length = taps_ref.shape
    blocks = length // LANES
    frames = own_ref.shape[1] // length
    past = taps - 1
    for ref, start in ((history_ref, 0), (own_ref, past * blocks)):

        def widen(step, carry, ref=ref, start=start):
            at = pl.multiple_of(step * (16 * LANES), 16 * LANES)
            piece = ref[:, pl.ds(at, 16 * LANES)]
            for j in range(16):
                wide[start + step * 16 + j] = piece[:, j * LANES : (j + 1) * LANES].astype(jnp.float32)
            return carry

        lax.fori_loop(0, ref.shape[1] // LANES // 16, widen, 0)

    def filter_block(block, carry):
        at = pl.multiple_of(block * LANES, LANES)
        weights = [
            jnp.broadcast_to(taps_ref[k : k + 1, pl.ds(at, LANES)], (rows, LANES)) for k in range(taps)
        ]
        values = [wide[frame * blocks + block] for frame in range(frames + past)]
        for frame in range(frames):
            total = values[frame + past] * weights[0]
            for k in range(1, taps):
                total = total + values[frame + past - k] * weights[k]
            summed[frame, pl.ds(block, rows, stride=blocks), :] = total
        return carry

    lax.fori_loop(0, blocks, filter_block, 0)
    height = rows * blocks
    per_group = height // GROUPS

    def transform(frame, carry):
        middle = dot(first_ref[...], summed[frame].astype(jnp.bfloat16))
        left_part, right_part = middle[:height], middle[height:]
        twist_cos, twist_sin = cos_ref[...], sin_ref[...]
        low = (left_part * twist_cos + right_part * twist_sin).astype(jnp.bfloat16)
        high = (right_part * twist_cos - left_part * twist_sin).astype(jnp.bfloat16)
        at = pl.multiple_of(frame * per_group, per_group)
        for i in range(GROUPS):
            here = slice(i * per_group, (i + 1) * per_group)
            twisted[i, pl.ds(at, per_group), :LANES] = low[here]
            twisted[i, pl.ds(at, per_group), LANES:] = high[here]
        return carry

    lax.fori_loop(0, frames, transform, 0)
    for i in range(GROUPS):
        mixed[i] = dot(twisted[i], second_ref[:, i * LANES : (i + 1) * LANES])
    group = lax.broadcasted_iota(jnp.int32, (rows, LANES), 1) // (LANES // GROUPS)

    def gather(step, carry):
        at = pl.multiple_of(step * rows, rows)
        tiles = [mixed[i, pl.ds(at, rows), :] for i in range(GROUPS)]
        for bit in (1, 2, 4):
            pick = (group & bit) != 0
            tiles = [jnp.where(pick, tiles[(i + bit) % GROUPS], tiles[i]) for i in range(GROUPS)]
        lane = pl.multiple_of(step * LANES, LANES)
        for d in range(GROUPS):
            out_ref[d * rows : (d + 1) * rows, pl.ds(lane, LANES)] = tiles[-d % GROUPS].astype(jnp.bfloat16)
        return carry

    lax.fori_loop(0, frames * blocks // GROUPS, gather, 0)


def correlator_spectra(history, own, taps):
    rows, samples = own.shape
    length = taps.shape[1]
    frames = samples // length
    blocks = length // LANES
    first = jnp.asarray(block_stage_table(blocks, rows // 2), jnp.bfloat16)
    second = jnp.asarray(lane_stage_table(), jnp.bfloat16)
    twist_cos, twist_sin = twiddle_tables(blocks, rows)
    height = rows * blocks
    tiles = frames * blocks // GROUPS
    return pl.pallas_call(
        correlator_kernel,
        out_shape=jax.ShapeDtypeStruct((GROUPS * rows, tiles * LANES), jnp.bfloat16),
        scratch_shapes=[
            pltpu.VMEM(((frames + taps.shape[0] - 1) * blocks, rows, LANES), jnp.float32),
            pltpu.VMEM((frames, height, LANES), jnp.float32),
            pltpu.VMEM((GROUPS, frames * height // GROUPS, 2 * LANES), jnp.bfloat16),
            pltpu.VMEM((GROUPS, frames * height // GROUPS, LANES), jnp.float32),
        ],
        cost_estimate=pl.CostEstimate(flops=10000000000, bytes_accessed=4000000, transcendentals=0),
        compiler_params=pltpu.CompilerParams(vmem_limit_bytes=VMEM_BYTES),
        name="correlator_spectra",
    )(history, own, taps, first, second, jnp.asarray(twist_cos), jnp.asarray(twist_sin))


def beam_kernel(weight_ref, spec_ref, out_ref, stacked):
    groups, depth, _ = stacked.shape
    members = depth // weight_ref.shape[2]
    sources = spec_ref.shape[0] // (members * groups)
    terms = weight_ref.shape[2] // sources
    width = spec_ref.shape[1] // terms
    height = weight_ref.shape[1] // groups
    frames = width // 2
    for term in range(terms):
        piece = spec_ref[:, term * width : (term + 1) * width]
        for source in range(sources):
            for group in range(groups):
                start = (source * groups + group) * members
                at = (term * sources + source) * members
                stacked[group, at : at + members, :] = piece[start : start + members]
    beams = height // members
    spread = lax.broadcasted_iota(jnp.int32, (weight_ref.shape[2], depth), 1) // members
    spread = (spread == lax.broadcasted_iota(jnp.int32, (weight_ref.shape[2], depth), 0)).astype(jnp.bfloat16)
    same = lax.broadcasted_iota(jnp.int32, (height, depth), 0) // beams
    same = same == lax.broadcasted_iota(jnp.int32, (height, depth), 1) % members
    for group in range(groups):
        power = None
        for part in range(2):
            rows = weight_ref[part, group * height : (group + 1) * height, :]
            wide = jnp.where(same, dot(rows, spread), 0.0).astype(jnp.bfloat16)
            field = dot(wide, stacked[group])
            power = field * field if power is None else power + field * field
        out_ref[group * height : (group + 1) * height, :] = power[:, :frames] + power[:, frames:]


def beam_former(weights, spectra, channels):
    _, height, terms = weights.shape
    members = min(channels, 16)
    groups = channels // members
    width = spectra.shape[1] * spectra.shape[0] // (terms * channels)
    return pl.pallas_call(
        beam_kernel,
        out_shape=jax.ShapeDtypeStruct((height, width // 2), jnp.float32),
        scratch_shapes=[pltpu.VMEM((groups, terms * members, width), jnp.bfloat16)],
        compiler_params=pltpu.CompilerParams(vmem_limit_bytes=VMEM_BYTES),
        cost_estimate=pl.CostEstimate(flops=4000000000, bytes_accessed=2000000, transcendentals=0),
        name="beam_former",
    )(weights, spectra)


def gram_kernel(spec_ref, out_ref):
    out_ref[...] = dot_rows(spec_ref[...], spec_ref[...])


def gram(spectra):
    rows = spectra.shape[0]
    return pl.pallas_call(
        gram_kernel,
        out_shape=jax.ShapeDtypeStruct((rows, rows), jnp.float32),
        cost_estimate=pl.CostEstimate(flops=2000000000, bytes_accessed=1000000, transcendentals=0),
        compiler_params=pltpu.CompilerParams(vmem_limit_bytes=VMEM_BYTES),
        name="gram",
    )(spectra)


def station_weights(index_rows, columns, station_total):
    table_rows = jnp.arange(columns.shape[0], dtype=jnp.int32)
    one_hot = (index_rows[..., None] == table_rows).astype(jnp.float32)
    angles = jnp.einsum("bst,tc->bsc", one_hot, columns, precision=lax.Precision.HIGHEST)
    factor = 1.0 / math.sqrt(station_total)
    return (
        (jnp.cos(angles) * factor).astype(jnp.bfloat16),
        (jnp.sin(angles) * factor).astype(jnp.bfloat16),
    )


def beam_rows(weight_real, weight_imag, local_stations):
    beams, stations, channels = weight_real.shape
    parts = jnp.stack(
        [jnp.stack([weight_real, -weight_imag], 0), jnp.stack([weight_imag, weight_real], 0)], 0
    )
    parts = parts.reshape(2, 2, beams, stations // local_stations, local_stations, channels)
    parts = parts.transpose(0, 5, 2, 1, 4, 3)
    return parts.reshape(2, channels * beams, 2 * stations)


def sum_over_grp(matrix):
    members = lax.axis_size("grp")
    me = lax.axis_index("grp")
    blocks = matrix.reshape(members, matrix.shape[0] // members, matrix.shape[1])
    total = lax.dynamic_index_in_dim(blocks, me, 0, keepdims=False)
    for by in range(1, members):
        away = lax.dynamic_index_in_dim(blocks, (me + by) % members, 0, keepdims=False)
        total = total + lax.ppermute(away, "grp", [(i, (i + by) % members) for i in range(members)])
    return total


def on_device(voltages, corr_taps, beam_taps, angle_table, table_index):
    tap_count = corr_taps.shape[0]
    length = corr_taps.shape[1]
    short_length = beam_taps.shape[1]
    local_stations, polarizations, samples = voltages.shape[1:]
    owners = lax.axis_size("stn")
    station_total = local_stations * owners
    pairs = local_stations * polarizations
    rows = 2 * pairs
    own = voltages.reshape(rows, samples)
    short_past = (tap_count - 1) * short_length
    near = from_behind(own[:, samples - short_past :], "grp", 1)
    past = from_behind(own[:, samples - (tap_count - 1) * length :], "grp", 1)
    short = pulsar_spectra(near, own, beam_taps)
    owned_channels = short_length // owners
    short = short.reshape(owners, owned_channels, short.shape[1])
    short_turned = lax.all_to_all(short, "stn", split_axis=0, concat_axis=0, tiled=True)
    spectra = correlator_spectra(past, own, corr_taps)
    subs = owners // GROUPS
    spectra = spectra.reshape(GROUPS, rows, -1, subs, LANES // GROUPS // subs)
    spectra = spectra.transpose(0, 3, 1, 2, 4).reshape(owners, rows, -1)
    turned = lax.all_to_all(spectra, "stn", split_axis=0, concat_axis=0, tiled=True)
    columns = lax.dynamic_slice_in_dim(
        angle_table, lax.axis_index("stn") * owned_channels, owned_channels, 1
    )
    weight_real, weight_imag = station_weights(table_index, columns, station_total)
    weights = beam_rows(weight_real, weight_imag, local_stations)
    beam_power = beam_former(weights, short_turned.reshape(owners * owned_channels, -1), owned_channels)
    beam_power = beam_power.reshape(owned_channels, table_index.shape[0], -1)
    inner_depth = turned.shape[2]
    products = gram(turned.reshape(owners * rows, inner_depth))
    summed = sum_over_grp(products)
    held = owners // lax.axis_size("grp")
    summed = summed.reshape(held, 2, pairs, owners, 2, pairs)
    real_part = summed[:, 0, :, :, 0] + summed[:, 1, :, :, 1]
    imag_part = summed[:, 1, :, :, 0] - summed[:, 0, :, :, 1]
    signals = owners * pairs
    visibility = jnp.stack(
        [real_part.reshape(held * pairs, signals), imag_part.reshape(held * pairs, signals)], 1
    )
    visibility = (visibility * (1.0 / math.sqrt(inner_depth * lax.axis_size("grp"))))[None]
    return (visibility, beam_power)


def solution(mesh):
    in_specs = (P(None, "stn", None, "grp"), P(), P(), P(), P())
    out_specs = (P("stn", "grp", None, None), P("stn", None, "grp"))
    return jax.shard_map(on_device, mesh=mesh, in_specs=in_specs, out_specs=out_specs, check_vma=False)
```

```python
import functools
import math

import jax
import jax.numpy as jnp
import numpy as np
from jax import lax
from jax.experimental import pallas as pl
from jax.experimental.pallas import tpu as pltpu
from jax.sharding import PartitionSpec as P

LANES = 128
GROUPS = 8
CROSS = (6, 7, 4, 5)
NEAR = (2, 3, 1)
VMEM_BYTES = 24 * 1024 * 1024


def from_behind(array, axis, by):
    devices = lax.axis_size(axis)
    pairs = [(i, i + by) for i in range(devices) if 0 <= i + by < devices]
    return lax.ppermute(array, axis, pairs)


def dft_tables(rows, columns):
    length = max(rows, columns)
    phases = (np.arange(rows)[:, None] * np.arange(columns)[None, :] % length) * (2.0 * np.pi / length)
    return np.cos(phases) / math.sqrt(length), np.sin(phases) / math.sqrt(length)


def pulsar_table(length):
    cos_table, sin_table = dft_tables(length, length)
    return np.concatenate([cos_table, sin_table], 1)


def block_stage_table(blocks, pairs):
    cos_table, sin_table = dft_tables(blocks, blocks)
    real_row = np.stack([cos_table, sin_table], 0)
    imag_row = np.stack([-sin_table, cos_table], 0)
    parts = np.stack([np.stack([real_row, imag_row], 0), np.stack([imag_row, -real_row], 0)], 0)
    parts = parts.reshape(2, 2, 2, blocks, blocks // GROUPS, GROUPS)
    full = np.einsum("aorbqi,sp->aiqosrpb", parts, np.eye(pairs))
    return full.reshape(2 * blocks * 2 * pairs, 2 * pairs * blocks)


def lane_stage_table():
    cos_table, sin_table = dft_tables(LANES, LANES)
    table = np.concatenate([cos_table, sin_table], 0)
    width = LANES // GROUPS
    return np.concatenate([np.roll(table, i * width, 1) for i in range(GROUPS)], 1)


def twiddle_tables(blocks, repeats):
    order = np.arange(blocks).reshape(blocks // GROUPS, GROUPS).T.reshape(-1)
    phases = (order[:, None] * np.arange(LANES)[None, :]) * (2.0 * np.pi / (blocks * LANES))
    phases = np.repeat(phases, repeats, 0)
    return np.cos(phases).astype(np.float32), np.sin(phases).astype(np.float32)


def dot(left_side, right_side):
    return jnp.dot(left_side, right_side, preferred_element_type=jnp.float32)


def dot_rows(left_side, right_side):
    return lax.dot_general(
        left_side, right_side, (((1,), (1,)), ((), ())), preferred_element_type=jnp.float32
    )


def pulsar_kernel(me_ref, history_ref, own_ref, taps_ref, table_ref, *refs):
    out_refs, (wide, summed, stacked, turned) = refs[:GROUPS], refs[GROUPS:]
    rows = own_ref.shape[0]
    taps, length = taps_ref.shape
    parts = length // LANES
    frames = own_ref.shape[1] // length
    past = history_ref.shape[1] // LANES
    for block in range(past):
        wide[block] = history_ref[:, block * LANES : (block + 1) * LANES].astype(jnp.float32)

    def widen(step, carry):
        at = pl.multiple_of(step * (16 * LANES), 16 * LANES)
        piece = own_ref[:, pl.ds(at, 16 * LANES)]
        for j in range(16):
            wide[past + step * 16 + j] = piece[:, j * LANES : (j + 1) * LANES].astype(jnp.float32)
        return carry

    lax.fori_loop(0, own_ref.shape[1] // LANES // 16, widen, 0)
    chunk = 16
    for part in range(parts):
        weights = [
            jnp.broadcast_to(taps_ref[k : k + 1, part * LANES : (part + 1) * LANES], (rows, LANES))
            for k in range(taps)
        ]

        def filter_frames(step, carry):
            first = step * chunk
            values = [wide[(first + j) * parts + part] for j in range(chunk + taps - 1)]
            for j in range(chunk):
                total = values[j + taps - 1] * weights[0]
                for k in range(1, taps):
                    total = total + values[j + taps - 1 - k] * weights[k]
                summed[part, pl.ds(first + j, rows, stride=frames), :] = total
            return carry

        lax.fori_loop(0, frames // chunk, filter_frames, 0)
    half = rows * frames // 2

    def stack(step, carry):
        at = pl.multiple_of(step * 64, 64)
        for part in range(parts):
            real_part = summed[part, pl.ds(at, 64), :].astype(jnp.bfloat16)
            imag_part = summed[part, pl.ds(at + half, 64), :].astype(jnp.bfloat16)
            low = slice(part * LANES, (part + 1) * LANES)
            high = slice(length + part * LANES, length + (part + 1) * LANES)
            stacked[pl.ds(at, 64), low] = real_part
            stacked[pl.ds(at, 64), high] = imag_part
            stacked[pl.ds(at + half, 64), low] = imag_part
            stacked[pl.ds(at + half, 64), high] = -real_part
        return carry

    lax.fori_loop(0, half // 64, stack, 0)
    share = length // GROUPS
    for slot in range(GROUPS):
        at = pl.multiple_of((slot ^ me_ref[0]) * share, share)
        turned[slot * share : (slot + 1) * share, :] = table_ref[pl.ds(at, share), :]
    spectra = dot_rows(turned[...], stacked[...]).astype(jnp.bfloat16)
    for slot in range(GROUPS):
        out_refs[slot][...] = spectra[slot * share : (slot + 1) * share]


def on_chip(count):
    return [pl.BlockSpec(memory_space=pltpu.SMEM)] + [pl.BlockSpec(memory_space=pltpu.VMEM)] * count


def pulsar_spectra(me, history, own, taps):
    rows, samples = own.shape
    length = taps.shape[1]
    frames = samples // length
    table = jnp.asarray(pulsar_table(length), jnp.bfloat16)
    blocks = (history.shape[1] + samples) // LANES
    return pl.pallas_call(
        pulsar_kernel,
        out_shape=[jax.ShapeDtypeStruct((length // GROUPS, rows * frames), jnp.bfloat16)] * GROUPS,
        in_specs=on_chip(4),
        scratch_shapes=[
            pltpu.VMEM((blocks, rows, LANES), jnp.float32),
            pltpu.VMEM((length // LANES, rows * frames, LANES), jnp.float32),
            pltpu.VMEM((rows * frames, 2 * length), jnp.bfloat16),
            pltpu.VMEM((length, 2 * length), jnp.bfloat16),
        ],
        cost_estimate=pl.CostEstimate(flops=5000000000, bytes_accessed=2000000, transcendentals=0),
        compiler_params=pltpu.CompilerParams(vmem_limit_bytes=VMEM_BYTES),
        name="pulsar_spectra",
    )(me, history, own, taps, table)


def correlator_kernel(me_ref, history_ref, own_ref, taps_ref, first_ref, second_ref, cos_ref, sin_ref, *refs):
    out_refs, (wide, summed, twisted, mixed) = refs[:GROUPS], refs[GROUPS:]
    rows = own_ref.shape[0]
    taps, length = taps_ref.shape
    blocks = length // LANES
    frames = own_ref.shape[1] // length
    past = taps - 1
    for ref, start in ((history_ref, 0), (own_ref, past * blocks)):

        def widen(step, carry, ref=ref, start=start):
            at = pl.multiple_of(step * (16 * LANES), 16 * LANES)
            piece = ref[:, pl.ds(at, 16 * LANES)]
            for j in range(16):
                wide[start + step * 16 + j] = piece[:, j * LANES : (j + 1) * LANES].astype(jnp.float32)
            return carry

        lax.fori_loop(0, ref.shape[1] // LANES // 16, widen, 0)

    def filter_block(block, carry):
        at = pl.multiple_of(block * LANES, LANES)
        weights = [
            jnp.broadcast_to(taps_ref[k : k + 1, pl.ds(at, LANES)], (rows, LANES)) for k in range(taps)
        ]
        values = [wide[frame * blocks + block] for frame in range(frames + past)]
        for frame in range(frames):
            total = values[frame + past] * weights[0]
            for k in range(1, taps):
                total = total + values[frame + past - k] * weights[k]
            summed[frame, pl.ds(block, rows, stride=blocks), :] = total
        return carry

    lax.fori_loop(0, blocks, filter_block, 0)
    height = rows * blocks
    per_group = height // GROUPS

    def transform(frame, carry):
        middle = dot(first_ref[...], summed[frame].astype(jnp.bfloat16))
        left_part, right_part = middle[:height], middle[height:]
        twist_cos, twist_sin = cos_ref[...], sin_ref[...]
        low = (left_part * twist_cos + right_part * twist_sin).astype(jnp.bfloat16)
        high = (right_part * twist_cos - left_part * twist_sin).astype(jnp.bfloat16)
        at = pl.multiple_of(frame * per_group, per_group)
        for i in range(GROUPS):
            here = slice(i * per_group, (i + 1) * per_group)
            twisted[i, pl.ds(at, per_group), :LANES] = low[here]
            twisted[i, pl.ds(at, per_group), LANES:] = high[here]
        return carry

    lax.fori_loop(0, frames, transform, 0)
    for i in range(GROUPS):
        mixed[i] = dot(twisted[i], second_ref[:, i * LANES : (i + 1) * LANES])
    group = lax.broadcasted_iota(jnp.int32, (rows, LANES), 1) // (LANES // GROUPS)
    swap = {bit: jnp.full((rows, LANES), me_ref[0] & bit, jnp.int32) != 0 for bit in (1, 2, 4)}

    def gather(step, carry):
        at = pl.multiple_of(step * rows, rows)
        tiles = [mixed[i, pl.ds(at, rows), :] for i in range(GROUPS)]
        for bit in (1, 2, 4):
            pick = (group & bit) != 0
            tiles = [jnp.where(pick, tiles[(i + bit) % GROUPS], tiles[i]) for i in range(GROUPS)]
        tiles = [tiles[-d % GROUPS] for d in range(GROUPS)]
        for bit in (1, 2, 4):
            pick = swap[bit]
            tiles = [jnp.where(pick, tiles[d ^ bit], tiles[d]) for d in range(GROUPS)]
        lane = pl.multiple_of(step * LANES, LANES)
        for slot in range(GROUPS):
            out_refs[slot][:, pl.ds(lane, LANES)] = tiles[slot].astype(jnp.bfloat16)
        return carry

    lax.fori_loop(0, frames * blocks // GROUPS, gather, 0)


def correlator_spectra(me, history, own, taps):
    rows, samples = own.shape
    length = taps.shape[1]
    frames = samples // length
    blocks = length // LANES
    first = jnp.asarray(block_stage_table(blocks, rows // 2), jnp.bfloat16)
    second = jnp.asarray(lane_stage_table(), jnp.bfloat16)
    twist_cos, twist_sin = twiddle_tables(blocks, rows)
    height = rows * blocks
    tiles = frames * blocks // GROUPS
    return pl.pallas_call(
        correlator_kernel,
        out_shape=[jax.ShapeDtypeStruct((rows, tiles * LANES), jnp.bfloat16)] * GROUPS,
        in_specs=on_chip(7),
        scratch_shapes=[
            pltpu.VMEM(((frames + taps.shape[0] - 1) * blocks, rows, LANES), jnp.float32),
            pltpu.VMEM((frames, height, LANES), jnp.float32),
            pltpu.VMEM((GROUPS, frames * height // GROUPS, 2 * LANES), jnp.bfloat16),
            pltpu.VMEM((GROUPS, frames * height // GROUPS, LANES), jnp.float32),
        ],
        cost_estimate=pl.CostEstimate(flops=10000000000, bytes_accessed=4000000, transcendentals=0),
        compiler_params=pltpu.CompilerParams(vmem_limit_bytes=VMEM_BYTES),
        name="correlator_spectra",
    )(me, history, own, taps, first, second, jnp.asarray(twist_cos), jnp.asarray(twist_sin))


def beam_kernel(me_ref, weight_ref, *refs):
    spec_refs, (out_ref, stacked) = refs[:GROUPS], refs[GROUPS:]
    groups, depth, width = stacked.shape
    members = depth // weight_ref.shape[2]
    sources = spec_refs[0].shape[0] // (members * groups)
    terms = spec_refs[0].shape[1] // width
    height = weight_ref.shape[1] // groups
    frames = width // 2
    for term in range(terms):
        for slot in range(GROUPS):
            piece = spec_refs[slot][:, term * width : (term + 1) * width]
            for source in range(sources):
                for group in range(groups):
                    start = (source * groups + group) * members
                    at = ((term * GROUPS + slot) * sources + source) * members
                    if members % 8 == 0:
                        place = (term * GROUPS + (slot ^ me_ref[0])) * sources + source
                        at = pl.multiple_of(place * members, members)
                    stacked[group, pl.ds(at, members), :] = piece[start : start + members]
    beams = height // members
    spread = lax.broadcasted_iota(jnp.int32, (weight_ref.shape[2], depth), 1) // members
    spread = (spread == lax.broadcasted_iota(jnp.int32, (weight_ref.shape[2], depth), 0)).astype(jnp.bfloat16)
    same = lax.broadcasted_iota(jnp.int32, (height, depth), 0) // beams
    same = same == lax.broadcasted_iota(jnp.int32, (height, depth), 1) % members
    for group in range(groups):
        power = None
        for part in range(2):
            rows = weight_ref[part, group * height : (group + 1) * height, :]
            wide = jnp.where(same, dot(rows, spread), 0.0).astype(jnp.bfloat16)
            field = dot(wide, stacked[group])
            power = field * field if power is None else power + field * field
        out_ref[group * height : (group + 1) * height, :] = power[:, :frames] + power[:, frames:]


def beam_former(me, weights, spectra, channels):
    _, height, terms = weights.shape
    members = min(channels, 16)
    groups = channels // members
    width = GROUPS * spectra[0].shape[1] * spectra[0].shape[0] // (terms * channels)
    return pl.pallas_call(
        beam_kernel,
        out_shape=jax.ShapeDtypeStruct((height, width // 2), jnp.float32),
        in_specs=on_chip(1 + GROUPS),
        scratch_shapes=[pltpu.VMEM((groups, terms * members, width), jnp.bfloat16)],
        compiler_params=pltpu.CompilerParams(vmem_limit_bytes=VMEM_BYTES),
        cost_estimate=pl.CostEstimate(flops=4000000000, bytes_accessed=2000000, transcendentals=0),
        name="beam_former",
    )(me, weights, *spectra)


def gram_kernel(*refs):
    spectra = jnp.concatenate([ref[...] for ref in refs[:GROUPS]], 0)
    refs[GROUPS][...] = dot_rows(spectra, spectra)


def gram(spectra):
    rows = GROUPS * spectra[0].shape[0]
    return pl.pallas_call(
        gram_kernel,
        out_shape=jax.ShapeDtypeStruct((rows, rows), jnp.float32),
        compiler_params=pltpu.CompilerParams(vmem_limit_bytes=VMEM_BYTES),
        cost_estimate=pl.CostEstimate(flops=2000000000, bytes_accessed=1000000, transcendentals=0),
        name="gram",
    )(*spectra)


def finish_kernel(pairs, scale, me_ref, *refs):
    out_ref = refs[-1]
    total = refs[0][...]
    for ref in refs[1:-1]:
        total = total + ref[...]
    rows, columns = total.shape
    held = rows // (2 * pairs)
    signals = columns // 2
    at = lax.broadcasted_iota(jnp.int32, (columns, signals), 0)
    to = lax.broadcasted_iota(jnp.int32, (columns, signals), 1)
    source = (at // (2 * pairs)) ^ me_ref[0]
    wanted = source * pairs + at % pairs == to
    part = at // pairs % 2
    halves = []
    for value in (0, 1):
        pick = jnp.where(wanted & (part == value), scale, 0.0).astype(jnp.float32)
        halves.append(
            jnp.dot(total, pick, precision=lax.Precision.HIGHEST, preferred_element_type=jnp.float32)
        )
    for slot in range(held):
        first = slot * 2 * pairs
        real = slice(first, first + pairs)
        imag = slice(first + pairs, first + 2 * pairs)
        row = (slot ^ (me_ref[0] & (held - 1))) * pairs
        out_ref[0, pl.ds(row, pairs), 0, :] = halves[0][real] + halves[1][imag]
        out_ref[0, pl.ds(row, pairs), 1, :] = halves[0][imag] - halves[1][real]


def finish(me, blocks, pairs, scale):
    rows, columns = blocks[0].shape
    return pl.pallas_call(
        functools.partial(finish_kernel, pairs, scale),
        out_shape=jax.ShapeDtypeStruct((1, rows // 2, 2, columns // 2), jnp.float32),
        in_specs=on_chip(len(blocks)),
        compiler_params=pltpu.CompilerParams(vmem_limit_bytes=VMEM_BYTES),
        name="finish",
    )(me, *blocks)


def station_weights(index_rows, columns, station_total):
    table_rows = jnp.arange(columns.shape[0], dtype=jnp.int32)
    one_hot = (index_rows[..., None] == table_rows).astype(jnp.float32)
    angles = jnp.einsum("bst,tc->bsc", one_hot, columns, precision=lax.Precision.HIGHEST)
    factor = 1.0 / math.sqrt(station_total)
    return (
        (jnp.cos(angles) * factor).astype(jnp.bfloat16),
        (jnp.sin(angles) * factor).astype(jnp.bfloat16),
    )


def beam_rows(weight_real, weight_imag, local_stations):
    beams, stations, channels = weight_real.shape
    parts = jnp.stack(
        [jnp.stack([weight_real, -weight_imag], 0), jnp.stack([weight_imag, weight_real], 0)], 0
    )
    parts = parts.reshape(2, 2, beams, stations // local_stations, local_stations, channels)
    parts = parts.transpose(0, 5, 2, 1, 4, 3)
    return parts.reshape(2, channels * beams, 2 * stations)


def exchange(slots):
    turned = list(slots)
    for k in CROSS + NEAR:
        turned[k] = lax.ppermute(slots[k], "stn", [(i, i ^ k) for i in range(GROUPS)])
    return turned


def exchange_all(slots, owners):
    rows, columns = slots[0].shape
    whole = jnp.concatenate(slots, 0).reshape(owners, GROUPS * rows // owners, columns)
    whole = lax.all_to_all(whole, "stn", split_axis=0, concat_axis=0, tiled=True)
    whole = whole.reshape(GROUPS, rows, columns)
    return [whole[k] for k in range(GROUPS)]


def shares_of_grp(me, products):
    members = lax.axis_size("grp")
    here = lax.axis_index("grp")
    rows = products.shape[0] // members
    held = rows // (products.shape[0] // GROUPS) if rows * GROUPS > products.shape[0] else 1
    blocks = products.reshape(members, rows, products.shape[1])
    terms = []
    for by in range(members):
        block = ((here + by) % members) ^ (me // held)
        block = lax.dynamic_index_in_dim(blocks, block, 0, keepdims=False)
        if by:
            block = lax.ppermute(block, "grp", [(i, (i + by) % members) for i in range(members)])
        terms.append(block)
    return terms


def on_device(voltages, corr_taps, beam_taps, angle_table, table_index):
    tap_count = corr_taps.shape[0]
    length = corr_taps.shape[1]
    short_length = beam_taps.shape[1]
    local_stations, polarizations, samples = voltages.shape[1:]
    owners = lax.axis_size("stn")
    station_total = local_stations * owners
    pairs = local_stations * polarizations
    rows = 2 * pairs
    direct = owners == GROUPS and short_length // owners % 8 == 0
    me = lax.axis_index("stn") if direct else jnp.int32(0)
    me_array = jnp.reshape(me, (1,)).astype(jnp.int32)
    own = voltages.reshape(rows, samples)
    short_past = (tap_count - 1) * short_length
    near = from_behind(own[:, samples - short_past :], "grp", 1)
    past = from_behind(own[:, samples - (tap_count - 1) * length :], "grp", 1)
    short = pulsar_spectra(me_array, near, own, beam_taps)
    owned_channels = short_length // owners
    short = exchange(short) if direct else exchange_all(short, owners)
    spectra = correlator_spectra(me_array, past, own, corr_taps)
    if direct:
        turned = exchange(spectra)
    else:
        subs = owners // GROUPS
        spectra = [
            slot.reshape(rows, -1, subs, LANES // GROUPS // subs).transpose(2, 0, 1, 3).reshape(subs * rows, -1)
            for slot in spectra
        ]
        turned = exchange_all(spectra, owners)
    columns = lax.dynamic_slice_in_dim(
        angle_table, lax.axis_index("stn") * owned_channels, owned_channels, 1
    )
    weight_real, weight_imag = station_weights(table_index, columns, station_total)
    weights = beam_rows(weight_real, weight_imag, local_stations)
    beam_power = beam_former(me_array, weights, short, owned_channels)
    beam_power = beam_power.reshape(owned_channels, table_index.shape[0], -1)
    inner_depth = samples // length * (length // owners)
    products = gram(turned)
    terms = shares_of_grp(me, products)
    scale = 1.0 / math.sqrt(inner_depth * lax.axis_size("grp"))
    visibility = finish(me_array, terms, pairs, scale)
    return (visibility, beam_power)


def solution(mesh):
    in_specs = (P(None, "stn", None, "grp"), P(), P(), P(), P())
    out_specs = (P("stn", "grp", None, None), P("stn", None, "grp"))
    return jax.shard_map(on_device, mesh=mesh, in_specs=in_specs, out_specs=out_specs, check_vma=False)
```
